512 devices in a mesh: layer: 8 (over z), row: 64 (over y, x, core).
Axes of the slice: x: 4, y: 8, z: 8, core: 2. Of those that a mesh axis runs over, the one named last changes fastest.
Arguments:
- left_factors: bfloat16 [8, 65536, 128], P('layer', 'row'), may hold values from -0.1875 to 0.1875
- right_factors: bfloat16 [8, 65536, 128], P('layer', 'row'), may hold values from -0.1875 to 0.1875
- sketch: bfloat16 [65536, 128], P('row'), may hold values from -0.1875 to 0.1875
- row_basis: bfloat16 [65536, 128], P('row'), may hold values from -0.4375 to 0.4375
- inverse_diag: bfloat16 [65536, 1024], P('row'), may hold values from -0.0625 to 1.44125, as said below
- right_side: bfloat16 [65536, 4096], P('row', 'layer'), may hold values from -6 to 6
- incoming: float32 [128, 4096], P(None, 'layer'), may hold values from -6 to 6
Outputs:
- solution: bfloat16 [65536, 4096], P('row', 'layer')
The draws below stay inside these ranges and needn't reach their ends.
Inputs may be any that keep to these rules, and one draw needn't show every extreme that they name: `inverse_diag`: each block of 1024 rows is the inverse of that row group's diagonal tile.
All inputs are finite; a program needn't handle non-finite values.
Results may differ from the reference program's by a relative error of at most 0.0095.
Values may be sent and summed in bfloat16 or wider, within the bound.
A program may use at most 128 MiB of HBM per device.

```python
import math
import jax
import jax.numpy as jnp
from jax import lax

B = 1024
R = 128
LAYERS = 8
ROWS = 65536
COLS = 4096


def draw_inverse_diag(key, part):
    first, second = jax.random.split(jax.random.fold_in(key, 11))
    rows = lax.broadcasted_iota(jnp.int32, (ROWS, B), 0) % B
    cols = lax.broadcasted_iota(jnp.int32, (ROWS, B), 1)
    identity = (rows == cols).astype(jnp.float32)
    scale_diag = jax.random.uniform(first, (ROWS, 1), jnp.float32, 0.8, 1.2)
    spread = jnp.clip(jax.random.normal(second, (ROWS, B), jnp.float32), -4.0, 4.0) * (0.5 / math.sqrt(B))
    return (identity * scale_diag + spread).astype(jnp.bfloat16)


def steps_of(stream_key, extent, cuts, low, largest):
    factor_of = 1.0
    for axis_at, shards_of in cuts:
        steps = jax.random.uniform(jax.random.fold_in(jax.random.fold_in(stream_key, 6), axis_at), (shards_of,), jnp.float32, low / len(cuts), largest / len(cuts))
        factor_of = factor_of * jnp.repeat(jnp.exp(steps), extent[axis_at] // shards_of).reshape((-1,) + (1,) * (len(extent) - 1 - axis_at))
    return factor_of


def centred(rng, dims, scale, reach, shards=(), dtype=jnp.bfloat16):
    values = jax.random.normal(rng, dims, jnp.float32) * scale
    if len(shards) > 0:
        values = steps_of(rng, dims, shards, -0.22, 0.18) * values
    return jnp.clip(values, min=-reach, max=reach).astype(dtype)


def setup_inputs(seed: int = 0) -> dict:
    key_list = jax.random.split(jax.random.key(seed), 8)
    return {
        "left_factors": centred(key_list[0], (LAYERS, ROWS, R), (R * LAYERS) ** -0.5, 0.1875, ((0, 8), (1, 64))),
        "right_factors": centred(key_list[1], (LAYERS, ROWS, R), B ** -0.5, 0.1875, ((0, 8), (1, 64))),
        "sketch": centred(key_list[2], (ROWS, R), B ** -0.5, 0.1875, ((0, 64),)),
        "row_basis": centred(key_list[3], (ROWS, R), (R + R // 3) ** -0.5, 0.4375, ((0, 64),)),
        "inverse_diag": draw_inverse_diag(jax.random.fold_in(key_list[7], 71), 0),
        "right_side": centred(key_list[5], (ROWS, COLS), 1.0, 6.0, ((0, 64), (1, 8))),
        "incoming": centred(key_list[6], (R, COLS), 1.0, 6.0, ((1, 8),), jnp.float32),
    }


def reference(left_factors, right_factors, sketch, row_basis, inverse_diag, right_side, incoming):
    groups = ROWS // B
    full = lax.Precision.HIGHEST
    coupled = incoming.astype(jnp.float32)
    pieces = []
    for group in range(groups):
        lo = group * B
        hi = lo + B
        total = jnp.zeros((B, R), jnp.float32)
        for layer in range(LAYERS):
            core = jnp.dot(right_factors[layer, lo:hi].T, sketch[lo:hi], preferred_element_type=jnp.float32).astype(jnp.bfloat16)
            total = total - jnp.dot(left_factors[layer, lo:hi], core, preferred_element_type=jnp.float32)
        tile_range = total.astype(jnp.bfloat16)
        applied = jnp.dot(inverse_diag[lo:hi], right_side[lo:hi], preferred_element_type=jnp.float32).astype(jnp.bfloat16)
        gain = jnp.dot(inverse_diag[lo:hi], tile_range, preferred_element_type=jnp.float32).astype(jnp.bfloat16)
        result = applied.astype(jnp.float32) - jnp.dot(gain.astype(jnp.float32), coupled, precision=full)
        pieces.append(result.astype(jnp.bfloat16))
        if group + 1 < groups:
            basis = row_basis[hi:hi + B]
            step_map = -jnp.dot(basis.T, gain, preferred_element_type=jnp.float32)
            step_shift = jnp.dot(basis.T, applied, preferred_element_type=jnp.float32)
            coupled = jnp.dot(step_map, coupled, precision=full) + step_shift
    return jnp.concatenate(pieces, axis=0)
```

```python
import functools

import jax
import jax.numpy as jnp
from jax import lax
from jax.experimental import pallas as pl
from jax.experimental.pallas import tpu as pltpu
from jax.sharding import PartitionSpec as P

MESH = pl.DeviceIdType.MESH
INNER = 8
BF16 = jnp.bfloat16
F32 = jnp.float32


def mm(a, b, ca=1, cb=0):
    return lax.dot_general(a, b, (((ca,), (cb,)), ((), ())), preferred_element_type=F32)


def split(value):
    high = value.astype(BF16)
    return high, (value - high.astype(F32)).astype(BF16)


def far_first(n):
    return sorted(range(1, n), key=lambda o: -min(o, n - o))


RS, SH, MZ, GZ, MI, OU, CB, BS = range(8)


def kernel(
    nz, ni, ny,
    left, right, sketch, basis, inverse, rhs, incoming,
    out,
    v_left, v_right, v_sketch, v_basis, v_inv, v_invt, v_rhs, v_inc, v_app,
    part, part_in, shift, shift_in, maps, gain_t, gain, pre_s, pre_m, total, total_in,
    inc_t, carry, coup, coup_in,
    load_sem, send_sem, recv_sem,
):
    z, row = lax.axis_index("layer"), lax.axis_index("row")
    y, i = row // ni, row % ni
    rows = row - i
    n_row = ni * ny
    order, rank = v_inv.shape[0], v_sketch.shape[1]
    width = v_rhs.shape[1]
    cols = width // ni
    thick = rank // nz

    loads = [
        pltpu.make_async_copy(source, target, load_sem.at[k])
        for k, (source, target) in enumerate(
            [(right, v_right), (sketch, v_sketch), (left, v_left), (inverse, v_inv), (rhs, v_rhs), (incoming, v_inc)]
        )
    ]
    for load in loads:
        load.start()

    barrier = pltpu.get_barrier_semaphore()

    def greet(layer, target):
        pl.semaphore_signal(barrier, inc=1, device_id=(layer, target), device_id_type=MESH)

    for o in range(1, nz):
        greet((z + o) % nz, row)
    for o in range(1, ni):
        greet(z, rows + (i + o) % ni)
    for o in range(1, ny):
        greet(z, ((y + o) % ny) * ni + i)
    greet(z, (row + 1) % n_row)
    greet(z, (row + n_row - 1) % n_row)

    def send(kind, slot, source, target, layer, dest):
        copy = pltpu.make_async_remote_copy(
            src_ref=source,
            dst_ref=target,
            send_sem=send_sem.at[kind, slot],
            recv_sem=recv_sem.at[kind, slot],
            device_id=(layer, dest),
            device_id_type=MESH,
        )
        copy.start()
        return copy

    def await_slot(kind, slot, target):
        pltpu.make_async_remote_copy(
            src_ref=target,
            dst_ref=target,
            send_sem=send_sem.at[kind, slot],
            recv_sem=recv_sem.at[kind, slot],
            device_id=(z, row),
            device_id_type=MESH,
        ).wait_recv()

    sent = []

    loads[0].wait()
    loads[1].wait()
    core_t = mm(v_sketch[...], v_right[...], 0, 0).astype(BF16)
    loads[2].wait()
    part[...] = mm(core_t, v_left[...], 1, 1).reshape(part.shape)

    pl.semaphore_wait(barrier, (nz - 1) + (ni - 1) + (ny - 1) + 2)
    for o in far_first(nz):
        peer = (z + o) % nz
        sent.append(send(RS, o, part.at[peer], part_in.at[z], peer, row))
    sent.append(send(BS, 0, basis, v_basis, z, (row + n_row - 1) % n_row))

    for load in loads[3:]:
        load.wait()
    step = 256

    def apply_inverse(t, carried):
        at = pl.ds(pl.multiple_of(t * step, step), step)
        v_app[at, :] = mm(v_inv[at, :], v_rhs[...]).astype(BF16)
        return carried

    lax.fori_loop(0, order // step, apply_inverse, 0)
    await_slot(BS, 0, v_basis)
    step_shift = mm(v_basis[...], v_app[...], 0, 0)
    shift[...] = step_shift.T.reshape(shift.shape)
    for o in range(1, ni):
        peer = (i + o) % ni
        sent.append(send(SH, o, shift.at[peer], shift_in.at[i], z, rows + peer))
    shift_in[i] = shift[i]
    inc_t[...] = v_inc[...].T.reshape(inc_t.shape)

    for t in range(order // step):
        v_invt[:, t * step : (t + 1) * step] = v_inv[t * step : (t + 1) * step, :].T

    summed = part[z]
    for o in far_first(nz)[::-1]:
        source = (z + nz - o) % nz
        await_slot(RS, o, part_in.at[source])
        summed = summed + part_in[source]
    range_t = (-summed).astype(BF16)
    gain_part = mm(range_t, v_invt[...]).astype(BF16)
    gain_t[z] = gain_part
    high, low = split(-mm(gain_part, v_basis[...]))
    maps[i, z] = jnp.concatenate([high, low], axis=1)
    for o in far_first(nz):
        sent.append(send(MZ, o, maps.at[i, z], maps.at[i, z], (z + o) % nz, row))
    for o in far_first(nz):
        sent.append(send(GZ, o, gain_t.at[z], gain_t.at[z], (z + o) % nz, row))
    for o in far_first(nz)[::-1]:
        await_slot(MZ, o, maps.at[i, (z + nz - o) % nz])
    for o in range(1, ni):
        sent.append(send(MI, o, maps.at[i], maps.at[i], z, rows + (i + o) % ni))

    for o in range(1, ni):
        await_slot(SH, o, shift_in.at[(i + ni - o) % ni])

    def arrive(k):
        @pl.when(k != i)
        def _():
            await_slot(MI, (i + ni - k) % ni, maps.at[k])

    arrive(0)
    first = maps[0].reshape(rank, 2 * rank).astype(F32)
    state = jnp.concatenate([shift_in[0], first[:, :rank] + first[:, rank:]], axis=0)
    tall = cols + rank
    for k in range(1, ni):
        pre_s[k] = state[:cols]
        pre_m[:, k * rank : (k + 1) * rank] = state[cols:].astype(BF16)
        arrive(k)
        product = mm(jnp.concatenate(split(state), axis=0), maps[k].reshape(rank, 2 * rank))
        state = product[:tall, :rank] + (product[:tall, rank:] + product[tall:, :rank])
        state = jnp.concatenate([state[:cols] + shift_in[k], state[cols:]], axis=0)
    total[...] = state.astype(BF16)

    for d in range(ny - 1, 0, -1):

        @pl.when(y + d < ny)
        def _():
            send(OU, d, total, total_in.at[y], z, row + d * ni)

    for o in far_first(nz)[::-1]:
        await_slot(GZ, o, gain_t.at[(z + nz - o) % nz])
    gain[...] = gain_t[...].reshape(rank, order).T

    carry[...] = inc_t[i]
    for k in range(ny - 1):

        @pl.when(k < y)
        def _():
            await_slot(OU, y - k, total_in.at[k])
            product = mm(jnp.concatenate(split(carry[...]), axis=0), total_in[k, cols:, :])
            carry[...] = product[:cols] + product[cols:] + total_in[k, :cols, :].astype(F32)

    start = carry[...]
    coup[0] = start.astype(BF16)
    product = mm(jnp.concatenate(split(start), axis=0), pre_m[:, rank:])
    product = product[:cols] + product[cols:]
    for k in range(1, ni):
        coup[k] = (product[:, (k - 1) * rank : k * rank] + pre_s[k]).astype(BF16)
    for o in range(1, ni):
        peer = (i + o) % ni
        sent.append(send(CB, o, coup.at[peer], coup_in.at[i], z, rows + peer))
    coup_in[i] = coup[i]
    for o in range(1, ni):
        await_slot(CB, o, coup_in.at[(i + ni - o) % ni])

    coupled_t = coup_in[...].reshape(width, rank)
    for t in range(order // step):
        at = slice(t * step, (t + 1) * step)
        out[at, :] = (v_app[at, :].astype(F32) - mm(gain[at, :], coupled_t, 1, 1)).astype(BF16)

    for copy in sent:
        copy.wait_send()
    for d in range(1, ny):

        @pl.when(y + d < ny)
        def _():
            pltpu.make_async_remote_copy(
                src_ref=total,
                dst_ref=total_in.at[y],
                send_sem=send_sem.at[OU, d],
                recv_sem=recv_sem.at[OU, d],
                device_id=(z, row + d * ni),
                device_id_type=MESH,
            ).wait_send()


def solution(mesh, inner=INNER):
    nz, n_row = mesh.shape["layer"], mesh.shape["row"]
    ni, ny = inner, n_row // inner

    def body(left, right, sketch, row_basis, inverse, rhs, incoming):
        order, rank = sketch.shape
        width = rhs.shape[1]
        cols, thick = width // ni, rank // nz
        vm = pltpu.VMEM
        return pl.pallas_call(
            functools.partial(kernel, nz, ni, ny),
            out_shape=jax.ShapeDtypeStruct((order, width), BF16),
            in_specs=[pl.BlockSpec(memory_space=pltpu.HBM)] * 7,
            out_specs=pl.BlockSpec(memory_space=pltpu.VMEM),
            scratch_shapes=[
                vm((order, rank), BF16),
                vm((order, rank), BF16),
                vm((order, rank), BF16),
                vm((order, rank), BF16),
                vm((order, order), BF16),
                vm((order, order), BF16),
                vm((order, width), BF16),
                vm((rank, width), F32),
                vm((order, width), BF16),
                vm((nz, thick, order), F32),
                vm((nz, thick, order), F32),
                vm((ni, cols, rank), F32),
                vm((ni, cols, rank), F32),
                vm((ni, nz, thick, 2 * rank), BF16),
                vm((nz, thick, order), BF16),
                vm((order, rank), BF16),
                vm((ni, cols, rank), F32),
                vm((rank, ni * rank), BF16),
                vm((cols + rank, rank), BF16),
                vm((ny, cols + rank, rank), BF16),
                vm((ni, cols, rank), F32),
                vm((cols, rank), F32),
                vm((ni, cols, rank), BF16),
                vm((ni, cols, rank), BF16),
                pltpu.SemaphoreType.DMA((6,)),
                pltpu.SemaphoreType.DMA((8, 8)),
                pltpu.SemaphoreType.DMA((8, 8)),
            ],
            compiler_params=pltpu.CompilerParams(
                collective_id=0, has_side_effects=True, vmem_limit_bytes=48 << 20
            ),
        )(*[pltpu.with_memory_space_constraint(a, pltpu.HBM) for a in (left[0], right[0], sketch, row_basis, inverse, rhs, incoming)])

    return jax.shard_map(
        body,
        mesh=mesh,
        in_specs=(
            P("layer", "row", None),
            P("layer", "row", None),
            P("row", None),
            P("row", None),
            P("row", None),
            P("row", "layer"),
            P(None, "layer"),
        ),
        out_specs=P("row", "layer"),
        check_vma=False,
    )
```

```python
import functools

import jax
import jax.numpy as jnp
from jax import lax
from jax.experimental import pallas as pl
from jax.experimental.pallas import tpu as pltpu
from jax.sharding import PartitionSpec as P

MESH = pl.DeviceIdType.MESH
INNER = 8
CUTS = 1
BF16 = jnp.bfloat16
F32 = jnp.float32


def mm(a, b, ca=1, cb=0):
    return lax.dot_general(a, b, (((ca,), (cb,)), ((), ())), preferred_element_type=F32)


def split(value):
    high = value.astype(BF16)
    return high, (value - high.astype(F32)).astype(BF16)


def far_first(n):
    return sorted(range(1, n), key=lambda o: -min(o, n - o))


SH, MZ, GZ, MI, OU, CB, BS = range(7)


def kernel(
    nz, ni, ny,
    left, right, sketch, basis, inverse, rhs, incoming,
    out,
    v_left, v_right, v_sketch, v_basis, v_inv, v_invt, v_rhs, v_inc, v_app,
    part, ring_in, ring_out, shift, shift_in, maps, gain_t, gain, pre_s, pre_m, total, total_in,
    inc_t, carry, coup, coup_in,
    load_sem, send_sem, recv_sem, ring_send, ring_recv,
):
    z, row = lax.axis_index("layer"), lax.axis_index("row")
    y, i = row // ni, row % ni
    rows = row - i
    n_row = ni * ny
    order, rank = v_inv.shape[0], v_sketch.shape[1]
    width = v_rhs.shape[1]
    cols = width // ni
    thick = rank // nz

    loads = [
        pltpu.make_async_copy(source, target, load_sem.at[k])
        for k, (source, target) in enumerate(
            [(right, v_right), (sketch, v_sketch), (left, v_left), (inverse, v_inv), (rhs, v_rhs), (incoming, v_inc)]
        )
    ]
    for load in loads:
        load.start()

    barrier = pltpu.get_barrier_semaphore()

    def greet(layer, target):
        pl.semaphore_signal(barrier, inc=1, device_id=(layer, target), device_id_type=MESH)

    for o in range(1, nz):
        greet((z + o) % nz, row)
    for o in range(1, ni):
        greet(z, rows + (i + o) % ni)
    for o in range(1, ny):
        greet(z, ((y + o) % ny) * ni + i)
    greet(z, (row + 1) % n_row)
    greet(z, (row + n_row - 1) % n_row)

    def send(kind, slot, source, target, layer, dest):
        copy = pltpu.make_async_remote_copy(
            src_ref=source,
            dst_ref=target,
            send_sem=send_sem.at[kind, slot],
            recv_sem=recv_sem.at[kind, slot],
            device_id=(layer, dest),
            device_id_type=MESH,
        )
        copy.start()
        return copy

    def await_slot(kind, slot, target):
        pltpu.make_async_remote_copy(
            src_ref=target,
            dst_ref=target,
            send_sem=send_sem.at[kind, slot],
            recv_sem=recv_sem.at[kind, slot],
            device_id=(z, row),
            device_id_type=MESH,
        ).wait_recv()

    sent = []

    loads[0].wait()
    loads[1].wait()
    core_t = mm(v_sketch[...], v_right[...], 0, 0).astype(BF16)
    loads[2].wait()
    part[...] = mm(core_t, v_left[...], 1, 1).reshape(part.shape)

    pl.semaphore_wait(barrier, (nz - 1) + (ni - 1) + (ny - 1) + 2)
    piece = order // CUTS

    def ring_views(way, far, half, cut):
        rows_at, cols_at = pl.ds(half * (thick // 2), thick // 2), pl.ds(cut * piece, piece)
        owner = (z + far) % nz if way == 0 else (z + nz - far) % nz
        return (
            part.at[owner, rows_at, cols_at],
            ring_out.at[way, far - 1, rows_at, cols_at],
            ring_in.at[way, far - 1, rows_at, cols_at],
        )

    def ring_copy(way, far, half, cut, source):
        return pltpu.make_async_remote_copy(
            src_ref=source,
            dst_ref=ring_views(way, far, half, cut)[2],
            send_sem=ring_send.at[way, far - 1, half * CUTS + cut],
            recv_sem=ring_recv.at[way, far - 1, half * CUTS + cut],
            device_id=((z + 1) % nz if way == 0 else (z + nz - 1) % nz, row),
            device_id_type=MESH,
        )

    longest, shortest = nz // 2, (nz - 1) // 2
    chains = [(way, half, longest if way == half else shortest) for way, half in ((0, 0), (1, 1), (0, 1), (1, 0))]

    def ring_round(turn):
        for way, half, most in chains:
            far = most - turn
            if far < 1:
                continue
            for cut in range(CUTS):
                own, staged, _ = ring_views(way, far, half, cut)
                if turn == 0:
                    source = own
                else:
                    ring_copy(way, far + 1, half, cut, own).wait_recv()
                    staged[...] = ring_views(way, far + 1, half, cut)[2][...] + own[...]
                    source = staged
                copy = ring_copy(way, far, half, cut, source)
                copy.start()
                sent.append(copy)

    ring_round(0)
    sent.append(send(BS, 0, basis, v_basis, z, (row + n_row - 1) % n_row))

    for load in loads[3:]:
        load.wait()
    step = 256

    def apply_inverse(t, carried):
        at = pl.ds(pl.multiple_of(t * step, step), step)
        v_app[at, :] = mm(v_inv[at, :], v_rhs[...]).astype(BF16)
        return carried

    lax.fori_loop(0, order // step, apply_inverse, 0)
    ring_round(1)
    for t in range(order // step):
        v_invt[:, t * step : (t + 1) * step] = v_inv[t * step : (t + 1) * step, :].T
    inc_t[...] = v_inc[...].T.reshape(inc_t.shape)
    ring_round(2)
    await_slot(BS, 0, v_basis)
    step_shift = mm(v_basis[...], v_app[...], 0, 0)
    shift[...] = step_shift.T.reshape(shift.shape)
    for o in range(1, ni):
        peer = (i + o) % ni
        sent.append(send(SH, o, shift.at[peer], shift_in.at[i], z, rows + peer))
    shift_in[i] = shift[i]
    for turn in range(3, longest):
        ring_round(turn)
    for way, half, most in chains[::-1]:
        if most > 0:
            for cut in range(CUTS):
                own, _, arrived = ring_views(way, 1, half, cut)
                ring_copy(way, 1, half, cut, own).wait_recv()
    summed = part[z]
    for way in range(2):
        halves = [
            ring_in[way, 0, half * (thick // 2) : (half + 1) * (thick // 2), :]
            if (longest if way == half else shortest) > 0
            else jnp.zeros((thick // 2, order), F32)
            for half in range(2)
        ]
        summed = summed + jnp.concatenate(halves, axis=0)
    range_t = (-summed).astype(BF16)
    gain_part = mm(range_t, v_invt[...]).astype(BF16)
    gain_t[z] = gain_part
    high, low = split(-mm(gain_part, v_basis[...]))
    maps[i, z] = jnp.concatenate([high, low], axis=1)
    for o in far_first(nz):
        sent.append(send(MZ, o, maps.at[i, z], maps.at[i, z], (z + o) % nz, row))
    for o in far_first(nz)[::-1]:
        await_slot(MZ, o, maps.at[i, (z + nz - o) % nz])
    for o in range(1, ni):
        sent.append(send(MI, o, maps.at[i], maps.at[i], z, rows + (i + o) % ni))
    for o in far_first(nz):
        sent.append(send(GZ, o, gain_t.at[z], gain_t.at[z], (z + o) % nz, row))

    for o in range(1, ni):
        await_slot(SH, o, shift_in.at[(i + ni - o) % ni])

    def arrive(k):
        @pl.when(k != i)
        def _():
            await_slot(MI, (i + ni - k) % ni, maps.at[k])

    arrive(0)
    first = maps[0].reshape(rank, 2 * rank).astype(F32)
    state = jnp.concatenate([shift_in[0], first[:, :rank] + first[:, rank:]], axis=0)
    tall = cols + rank
    for k in range(1, ni):
        pre_s[k] = state[:cols]
        pre_m[:, k * rank : (k + 1) * rank] = state[cols:].astype(BF16)
        arrive(k)
        product = mm(jnp.concatenate(split(state), axis=0), maps[k].reshape(rank, 2 * rank))
        state = product[:tall, :rank] + (product[:tall, rank:] + product[tall:, :rank])
        state = jnp.concatenate([state[:cols] + shift_in[k], state[cols:]], axis=0)
    total[...] = state.astype(BF16)
    carry[...] = inc_t[i]

    def follow(block, added):
        product = mm(jnp.concatenate(split(carry[...]), axis=0), block)
        return product[:cols] + product[cols:] + added

    def outer_copies(act):
        @pl.when(y == 0)
        def _():
            for d in range(ny - 1, 0, -1):
                act(d, total.at[pl.ds(0, cols)], total_in.at[0, pl.ds(0, cols)])

        for d in range(ny - 2, 0, -1):

            @pl.when(jnp.logical_and(y > 0, y + d < ny))
            def _():
                act(d, total, total_in.at[y])

    @pl.when(y == 0)
    def _():
        total[:cols, :] = follow(total[cols:, :], state[:cols]).astype(BF16)

    outer_copies(lambda d, source, target: send(OU, d, source, target, z, row + d * ni))

    for o in far_first(nz)[::-1]:
        await_slot(GZ, o, gain_t.at[(z + nz - o) % nz])
    gain[...] = gain_t[...].reshape(rank, order).T

    @pl.when(y > 0)
    def _():
        await_slot(OU, y, total_in.at[0, pl.ds(0, cols)])
        carry[...] = total_in[0, :cols, :].astype(F32)

    for k in range(1, ny - 1):

        @pl.when(k < y)
        def _():
            await_slot(OU, y - k, total_in.at[k])
            carry[...] = follow(total_in[k, cols:, :], total_in[k, :cols, :].astype(F32))

    start = carry[...]
    coup[0] = start.astype(BF16)
    product = mm(jnp.concatenate(split(start), axis=0), pre_m[:, rank:])
    product = product[:cols] + product[cols:]
    for k in range(1, ni):
        coup[k] = (product[:, (k - 1) * rank : k * rank] + pre_s[k]).astype(BF16)
    for o in range(1, ni):
        peer = (i + o) % ni
        sent.append(send(CB, o, coup.at[peer], coup_in.at[i], z, rows + peer))
    coup_in[i] = coup[i]
    for o in range(1, ni):
        await_slot(CB, o, coup_in.at[(i + ni - o) % ni])

    coupled_t = coup_in[...].reshape(width, rank)
    for t in range(order // step):
        at = slice(t * step, (t + 1) * step)
        out[at, :] = (v_app[at, :].astype(F32) - mm(gain[at, :], coupled_t, 1, 1)).astype(BF16)

    for copy in sent:
        copy.wait_send()
    def outer_sent(d, source, target):
        pltpu.make_async_remote_copy(
            src_ref=source,
            dst_ref=target,
            send_sem=send_sem.at[OU, d],
            recv_sem=recv_sem.at[OU, d],
            device_id=(z, row + d * ni),
            device_id_type=MESH,
        ).wait_send()

    outer_copies(outer_sent)


def solution(mesh, inner=INNER):
    nz, n_row = mesh.shape["layer"], mesh.shape["row"]
    ni, ny = inner, n_row // inner

    def body(left, right, sketch, row_basis, inverse, rhs, incoming):
        order, rank = sketch.shape
        width = rhs.shape[1]
        cols, thick = width // ni, rank // nz
        vm = pltpu.VMEM
        return pl.pallas_call(
            functools.partial(kernel, nz, ni, ny),
            out_shape=jax.ShapeDtypeStruct((order, width), BF16),
            in_specs=[pl.BlockSpec(memory_space=pltpu.HBM)] * 7,
            out_specs=pl.BlockSpec(memory_space=pltpu.VMEM),
            scratch_shapes=[
                vm((order, rank), BF16),
                vm((order, rank), BF16),
                vm((order, rank), BF16),
                vm((order, rank), BF16),
                vm((order, order), BF16),
                vm((order, order), BF16),
                vm((order, width), BF16),
                vm((rank, width), F32),
                vm((order, width), BF16),
                vm((nz, thick, order), F32),
                vm((2, max(nz // 2, 1), thick, order), F32),
                vm((2, max(nz // 2, 1), thick, order), F32),
                vm((ni, cols, rank), F32),
                vm((ni, cols, rank), F32),
                vm((ni, nz, thick, 2 * rank), BF16),
                vm((nz, thick, order), BF16),
                vm((order, rank), BF16),
                vm((ni, cols, rank), F32),
                vm((rank, ni * rank), BF16),
                vm((cols + rank, rank), BF16),
                vm((ny, cols + rank, rank), BF16),
                vm((ni, cols, rank), F32),
                vm((cols, rank), F32),
                vm((ni, cols, rank), BF16),
                vm((ni, cols, rank), BF16),
                pltpu.SemaphoreType.DMA((6,)),
                pltpu.SemaphoreType.DMA((8, 8)),
                pltpu.SemaphoreType.DMA((8, 8)),
                pltpu.SemaphoreType.DMA((2, 4, 2 * CUTS)),
                pltpu.SemaphoreType.DMA((2, 4, 2 * CUTS)),
            ],
            compiler_params=pltpu.CompilerParams(
                collective_id=0, has_side_effects=True, vmem_limit_bytes=48 << 20
            ),
        )(*[pltpu.with_memory_space_constraint(a, pltpu.HBM) for a in (left[0], right[0], sketch, row_basis, inverse, rhs, incoming)])

    return jax.shard_map(
        body,
        mesh=mesh,
        in_specs=(
            P("layer", "row", None),
            P("layer", "row", None),
            P("row", None),
            P("row", None),
            P("row", None),
            P("row", "layer"),
            P(None, "layer"),
        ),
        out_specs=P("row", "layer"),
        check_vma=False,
    )
```

```python
import functools

import jax
import jax.numpy as jnp
from jax import lax
from jax.experimental import pallas as pl
from jax.experimental.pallas import tpu as pltpu
from jax.sharding import PartitionSpec as P

MESH = pl.DeviceIdType.MESH
INNER = 8
BF16 = jnp.bfloat16
F32 = jnp.float32


def mm(a, b, ca=1, cb=0):
    return lax.dot_general(a, b, (((ca,), (cb,)), ((), ())), preferred_element_type=F32)


def split(value):
    high = value.astype(BF16)
    return high, (value - high.astype(F32)).astype(BF16)


def far_first(n):
    return sorted(range(1, n), key=lambda o: -min(o, n - o))


RS, SH, MZ, GZ, MI, OU, CB, BS, FW, ME = range(10)


def kernel(
    nz, ni, ny,
    left, right, sketch, basis, inverse, rhs, incoming,
    out,
    v_left, v_right, v_sketch, v_basis, v_inv, v_invt, v_rhs, v_inc, v_app,
    part, part_in, shift, shift_in, maps, gain_t, gain, pre_s, pre_m, total, total_in,
    inc_t, carry, coup, coup_in,
    block, merge_in, merged, load_sem, send_sem, recv_sem,
):
    z, row = lax.axis_index("layer"), lax.axis_index("row")
    y, i = row // ni, row % ni
    rows = row - i
    n_row = ni * ny
    order, rank = v_inv.shape[0], v_sketch.shape[1]
    width = v_rhs.shape[1]
    cols = width // ni
    thick = rank // nz

    loads = [
        pltpu.make_async_copy(source, target, load_sem.at[k])
        for k, (source, target) in enumerate(
            [(right, v_right), (sketch, v_sketch), (left, v_left), (inverse, v_inv), (rhs, v_rhs), (incoming, v_inc)]
        )
    ]
    for load in loads:
        load.start()

    barrier = pltpu.get_barrier_semaphore()

    def greet(layer, target):
        pl.semaphore_signal(barrier, inc=1, device_id=(layer, target), device_id_type=MESH)

    for o in range(1, nz):
        greet((z + o) % nz, row)
    for o in range(1, ni):
        greet(z, rows + (i + o) % ni)
    for o in range(1, ny):
        greet(z, ((y + o) % ny) * ni + i)
    greet(z, (row + 1) % n_row)
    greet(z, (row + n_row - 1) % n_row)

    def send(kind, slot, source, target, layer, dest):
        copy = pltpu.make_async_remote_copy(
            src_ref=source,
            dst_ref=target,
            send_sem=send_sem.at[kind, slot],
            recv_sem=recv_sem.at[kind, slot],
            device_id=(layer, dest),
            device_id_type=MESH,
        )
        copy.start()
        return copy

    def await_slot(kind, slot, target):
        pltpu.make_async_remote_copy(
            src_ref=target,
            dst_ref=target,
            send_sem=send_sem.at[kind, slot],
            recv_sem=recv_sem.at[kind, slot],
            device_id=(z, row),
            device_id_type=MESH,
        ).wait_recv()

    sent = []

    loads[0].wait()
    loads[1].wait()
    core_t = mm(v_sketch[...], v_right[...], 0, 0).astype(BF16)
    loads[2].wait()
    part[...] = mm(core_t, v_left[...], 1, 1).reshape(part.shape)

    pl.semaphore_wait(barrier, (nz - 1) + (ni - 1) + (ny - 1) + 2)

    merging = nz == 8
    thin = thick // 2
    low, high_rows = pl.ds(0, thin), pl.ds(thin, thin)

    def give(o):
        peer = (z + o) % nz
        send(RS, o, part.at[peer], part_in.at[z], peer, row)

    if merging:
        across = (z + 4) % nz
        sent.append(send(ME, 0, part.at[across, low], merge_in.at[0], (z + 1) % nz, row))
        sent.append(send(ME, 1, part.at[across, high_rows], merge_in.at[1], (z + 7) % nz, row))
        third, fifth = (z + 3) % nz, (z + 5) % nz
        send(RS, 3, part.at[third, high_rows], part_in.at[z, high_rows], third, row)
        send(RS, 5, part.at[fifth, low], part_in.at[z, low], fifth, row)
        give(2)
        give(6)
    else:
        for o in far_first(nz):
            give(o)
    sent.append(send(BS, 0, basis, v_basis, z, (row + n_row - 1) % n_row))

    for load in loads[3:]:
        load.wait()
    step = 256

    def apply_inverse(t, carried):
        at = pl.ds(pl.multiple_of(t * step, step), step)
        v_app[at, :] = mm(v_inv[at, :], v_rhs[...]).astype(BF16)
        return carried

    lax.fori_loop(0, order // step, apply_inverse, 0)
    for t in range(order // step):
        v_invt[:, t * step : (t + 1) * step] = v_inv[t * step : (t + 1) * step, :].T
    inc_t[...] = v_inc[...].T.reshape(inc_t.shape)
    if merging:
        await_slot(ME, 0, merge_in.at[0])
        merged[0] = merge_in[0] + part[third, :thin, :]
        send(RS, 3, merged.at[0], part_in.at[z, low], third, row)
        await_slot(ME, 1, merge_in.at[1])
        merged[1] = merge_in[1] + part[fifth, thin:, :]
        send(RS, 5, merged.at[1], part_in.at[z, high_rows], fifth, row)
        give(1)
        give(7)

    await_slot(BS, 0, v_basis)
    step_shift = mm(v_basis[...], v_app[...], 0, 0)
    shift[...] = step_shift.T.reshape(shift.shape)
    for o in range(1, ni):
        peer = (i + o) % ni
        sent.append(send(SH, o, shift.at[peer], shift_in.at[i], z, rows + peer))
    shift_in[i] = shift[i]

    summed = part[z]
    givers = [o for o in far_first(nz)[::-1] if not (merging and o == 4)]
    for o in givers:
        source = (z + nz - o) % nz
        await_slot(RS, o, part_in.at[source])
        summed = summed + part_in[source]
    range_t = (-summed).astype(BF16)
    gain_part = mm(range_t, v_invt[...]).astype(BF16)
    gain_t[z] = gain_part
    high, low = split(-mm(gain_part, v_basis[...]))
    maps[i, z] = jnp.concatenate([high, low], axis=1)
    for o in far_first(nz):
        sent.append(send(MZ, o, maps.at[i, z], maps.at[i, z], (z + o) % nz, row))

    def spread(layer):
        for o in far_first(ni):
            send(MI, o, maps.at[i, layer], maps.at[i, layer], z, rows + (i + o) % ni)

    spread(z)
    for o in far_first(nz)[::-1]:
        source = (z + nz - o) % nz
        await_slot(MZ, o, maps.at[i, source])
        spread(source)
    for o in far_first(nz):
        sent.append(send(GZ, o, gain_t.at[z], gain_t.at[z], (z + o) % nz, row))

    for o in range(1, ni):
        await_slot(SH, o, shift_in.at[(i + ni - o) % ni])

    def arrive(k):
        @pl.when(k != i)
        def _():
            await_slot(MI, (i + ni - k) % ni, maps.at[k])

    arrive(0)
    first = maps[0].reshape(rank, 2 * rank).astype(F32)
    state = jnp.concatenate([shift_in[0], first[:, :rank] + first[:, rank:]], axis=0)
    tall = cols + rank
    for k in range(1, ni):
        pre_s[k] = state[:cols]
        pre_m[:, k * rank : (k + 1) * rank] = state[cols:].astype(BF16)
        arrive(k)
        product = mm(jnp.concatenate(split(state), axis=0), maps[k].reshape(rank, 2 * rank))
        state = product[:tall, :rank] + (product[:tall, rank:] + product[tall:, :rank])
        state = jnp.concatenate([state[:cols] + shift_in[k], state[cols:]], axis=0)
    half = rank // 2
    shifts, core = pl.ds(half, cols), i % 2
    mine = pl.ds(pl.multiple_of(core * half, half), half + cols)
    map_mine = pl.ds(pl.multiple_of(core * (half + cols), half), half)
    total[:half, :] = state[cols : cols + half].astype(BF16)
    total[half : half + cols, :] = state[:cols].astype(BF16)
    total[half + cols :, :] = state[cols + half :].astype(BF16)
    carry[...] = inc_t[i]

    def matrix_of(rows):
        return jnp.concatenate([rows[:half], rows[half + cols :]], axis=0)

    def outer_copies(act):
        for d in far_first(ny):

            @pl.when(y == 0)
            def _():
                act(d, total.at[shifts], total_in.at[d, shifts])

            @pl.when(jnp.logical_and(y > 0, y + d < ny))
            def _():
                act(d, total.at[mine], total_in.at[d, mine])

    @pl.when(y == 0)
    def _():
        product = mm(jnp.concatenate(split(carry[...]), axis=0), matrix_of(total[...]))
        total[half : half + cols, :] = (product[:cols] + product[cols:] + state[:cols]).astype(BF16)

    def outer_sent(d, source, target):
        pltpu.make_async_remote_copy(
            src_ref=source,
            dst_ref=target,
            send_sem=send_sem.at[OU, d],
            recv_sem=recv_sem.at[OU, d],
            device_id=(z, row + d * ni),
            device_id_type=MESH,
        ).wait_send()

    outer_copies(lambda d, source, target: send(OU, d, source, target, z, row + d * ni))

    for o in far_first(nz)[::-1]:
        await_slot(GZ, o, gain_t.at[(z + nz - o) % nz])
    gain[...] = gain_t[...].reshape(rank, order).T

    def forward(d):
        return pltpu.make_async_remote_copy(
            src_ref=total_in.at[d, map_mine],
            dst_ref=total_in.at[d, map_mine],
            send_sem=send_sem.at[FW, d],
            recv_sem=recv_sem.at[FW, d],
            device_id=(z, row + 1 - 2 * core),
            device_id_type=MESH,
        )

    for d in range(1, ny):

        @pl.when(d < y)
        def _():
            await_slot(OU, d, total_in.at[d, mine])
            forward(d).start()

        near = d - 1
        if near < 1:
            continue

        @pl.when(near < y)
        def _():
            forward(near).wait_recv()
            matrix = matrix_of(total_in[near])
            if near == 1:
                block[:cols, :] = total_in[near, half : half + cols, :].astype(F32)
                block[cols:, :] = matrix.astype(F32)
            else:
                rows_in = jnp.concatenate([total_in[near, half : half + cols, :], matrix], axis=0)
                product = mm(rows_in, jnp.concatenate(split(block[cols:, :]), axis=1))
                product = product[:, :rank] + product[:, rank:]
                block[:cols, :] += product[:cols]
                block[cols:, :] = product[cols:]

    for d in range(1, ny):

        @pl.when(d == y)
        def _():
            await_slot(OU, d, total_in.at[d, shifts])
            if d == 1:
                carry[...] = total_in[d, half : half + cols, :].astype(F32)
            else:
                product = mm(total_in[d, half : half + cols, :], jnp.concatenate(split(block[cols:, :]), axis=1))
                carry[...] = product[:, :rank] + product[:, rank:] + block[:cols, :]

    start = carry[...]
    coup[0] = start.astype(BF16)
    product = mm(jnp.concatenate(split(start), axis=0), pre_m[:, rank:])
    product = product[:cols] + product[cols:]
    for k in range(1, ni):
        coup[k] = (product[:, (k - 1) * rank : k * rank] + pre_s[k]).astype(BF16)
    for o in far_first(ni):
        peer = (i + o) % ni
        sent.append(send(CB, o, coup.at[peer], coup_in.at[i], z, rows + peer))
    coup_in[i] = coup[i]
    for o in range(1, ni):
        await_slot(CB, o, coup_in.at[(i + ni - o) % ni])

    coupled_t = coup_in[...].reshape(width, rank)
    for t in range(order // step):
        at = slice(t * step, (t + 1) * step)
        out[at, :] = (v_app[at, :].astype(F32) - mm(gain[at, :], coupled_t, 1, 1)).astype(BF16)

    for copy in sent:
        copy.wait_send()
    def drain(kind, o, source):
        pltpu.make_async_remote_copy(
            src_ref=source,
            dst_ref=source,
            send_sem=send_sem.at[kind, o],
            recv_sem=recv_sem.at[kind, o],
            device_id=(z, row),
            device_id_type=MESH,
        ).wait_send()

    for o in givers:
        drain(RS, o, part.at[0])
    for o in range(1, ni):
        drain(MI, o, maps.at[i])

    outer_copies(outer_sent)
    for d in range(1, ny - 1):

        @pl.when(d < y)
        def _():
            forward(d).wait_send()


def solution(mesh, inner=INNER):
    nz, n_row = mesh.shape["layer"], mesh.shape["row"]
    ni, ny = inner, n_row // inner

    def body(left, right, sketch, row_basis, inverse, rhs, incoming):
        order, rank = sketch.shape
        width = rhs.shape[1]
        cols, thick = width // ni, rank // nz
        vm = pltpu.VMEM
        return pl.pallas_call(
            functools.partial(kernel, nz, ni, ny),
            out_shape=jax.ShapeDtypeStruct((order, width), BF16),
            in_specs=[pl.BlockSpec(memory_space=pltpu.HBM)] * 7,
            out_specs=pl.BlockSpec(memory_space=pltpu.VMEM),
            scratch_shapes=[
                vm((order, rank), BF16),
                vm((order, rank), BF16),
                vm((order, rank), BF16),
                vm((order, rank), BF16),
                vm((order, order), BF16),
                vm((order, order), BF16),
                vm((order, width), BF16),
                vm((rank, width), F32),
                vm((order, width), BF16),
                vm((nz, thick, order), F32),
                vm((nz, thick, order), F32),
                vm((ni, cols, rank), F32),
                vm((ni, cols, rank), F32),
                vm((ni, nz, thick, 2 * rank), BF16),
                vm((nz, thick, order), BF16),
                vm((order, rank), BF16),
                vm((ni, cols, rank), F32),
                vm((rank, ni * rank), BF16),
                vm((cols + rank, rank), BF16),
                vm((ny, cols + rank, rank), BF16),
                vm((ni, cols, rank), F32),
                vm((cols, rank), F32),
                vm((ni, cols, rank), BF16),
                vm((ni, cols, rank), BF16),
                vm((cols + rank, rank), F32),
                vm((2, max(thick // 2, 8), order), F32),
                vm((2, max(thick // 2, 8), order), F32),
                pltpu.SemaphoreType.DMA((6,)),
                pltpu.SemaphoreType.DMA((10, 8)),
                pltpu.SemaphoreType.DMA((10, 8)),
            ],
            compiler_params=pltpu.CompilerParams(
                collective_id=0, has_side_effects=True, vmem_limit_bytes=48 << 20
            ),
        )(*[pltpu.with_memory_space_constraint(a, pltpu.HBM) for a in (left[0], right[0], sketch, row_basis, inverse, rhs, incoming)])

    return jax.shard_map(
        body,
        mesh=mesh,
        in_specs=(
            P("layer", "row", None),
            P("layer", "row", None),
            P("row", None),
            P("row", None),
            P("row", None),
            P("row", "layer"),
            P(None, "layer"),
        ),
        out_specs=P("row", "layer"),
        check_vma=False,
    )
```

```python
import functools

import jax
import jax.numpy as jnp
from jax import lax
from jax.experimental import pallas as pl
from jax.experimental.pallas import tpu as pltpu
from jax.sharding import PartitionSpec as P

MESH = pl.DeviceIdType.MESH
INNER = 8
BF16 = jnp.bfloat16
F32 = jnp.float32


def mm(a, b, ca=1, cb=0):
    return lax.dot_general(a, b, (((ca,), (cb,)), ((), ())), preferred_element_type=F32)


def split(value):
    high = value.astype(BF16)
    return high, (value - high.astype(F32)).astype(BF16)


def far_first(n):
    return sorted(range(1, n), key=lambda o: -min(o, n - o))


RS, SH, GZ, CB, BS, ME, MZ, MI, OU, FW = range(10)
SEND_AT = [0, 1, 2, 3, 4, 5, 6, 7, 8, 16]
RECV_AT = [0, 1, 2, 3, 4, 5, 7, 15, 23, 31]


def kernel(
    nz, ni, ny,
    left, right, sketch, basis, inverse, rhs, incoming,
    out,
    v_left, v_right, v_sketch, v_basis, v_inv, v_invt, v_rhs, v_inc, v_app,
    part, part_in, shift, shift_in, maps, gain_t, gain, pre_s, pre_m, total, total_in,
    inc_t, carry, coup, coup_in,
    block, merge_in, merged, load_sem, send_sem, recv_sem,
):
    z, row = lax.axis_index("layer"), lax.axis_index("row")
    y, i = row // ni, row % ni
    rows = row - i
    n_row = ni * ny
    order, rank = v_inv.shape[0], v_sketch.shape[1]
    width = v_rhs.shape[1]
    cols = width // ni
    thick = rank // nz

    barrier = pltpu.get_barrier_semaphore()

    def greet(layer, target):
        pl.semaphore_signal(barrier, inc=1, device_id=(layer, target), device_id_type=MESH)

    for o in range(1, nz):
        greet((z + o) % nz, row)
    for o in range(1, ni):
        greet(z, rows + (i + o) % ni)
    for o in range(1, ny):
        greet(z, ((y + o) % ny) * ni + i)
    greet(z, (row + 1) % n_row)
    greet(z, (row + n_row - 1) % n_row)

    loads = [
        pltpu.make_async_copy(source, target, load_sem.at[k])
        for k, (source, target) in enumerate(
            [(right, v_right), (sketch, v_sketch), (left, v_left), (inverse, v_inv), (rhs, v_rhs), (incoming, v_inc)]
        )
    ]
    for load in loads:
        load.start()

    def semaphores(kind, slot):
        sent_at = SEND_AT[kind] + (slot if kind in (OU, FW) else 0)
        got_at = RECV_AT[kind] + (slot if kind in (ME, MZ, MI, OU, FW) else 0)
        return {"send_sem": send_sem.at[sent_at], "recv_sem": recv_sem.at[got_at]}

    def send(kind, slot, source, target, layer, dest):
        copy = pltpu.make_async_remote_copy(
            src_ref=source,
            dst_ref=target,
            **semaphores(kind, slot),
            device_id=(layer, dest),
            device_id_type=MESH,
        )
        copy.start()
        return copy

    def await_slot(kind, slot, target):
        pltpu.make_async_remote_copy(
            src_ref=target,
            dst_ref=target,
            **semaphores(kind, slot),
            device_id=(z, row),
            device_id_type=MESH,
        ).wait_recv()

    loads[0].wait()
    loads[1].wait()
    core_t = mm(v_sketch[...], v_right[...], 0, 0).astype(BF16)
    loads[2].wait()
    part[...] = mm(core_t, v_left[...], 1, 1).reshape(part.shape)

    pl.semaphore_wait(barrier, (nz - 1) + (ni - 1) + (ny - 1) + 2)

    merging = nz == 8
    thin = thick // 2
    low, high_rows = pl.ds(0, thin), pl.ds(thin, thin)

    def give(o):
        peer = (z + o) % nz
        send(RS, o, part.at[peer], part_in.at[z], peer, row)

    if merging:
        across = (z + 4) % nz
        send(ME, 0, part.at[across, low], merge_in.at[0], (z + 1) % nz, row)
        send(ME, 1, part.at[across, high_rows], merge_in.at[1], (z + 7) % nz, row)
        third, fifth = (z + 3) % nz, (z + 5) % nz
        send(RS, 3, part.at[third, high_rows], part_in.at[z, high_rows], third, row)
        send(RS, 5, part.at[fifth, low], part_in.at[z, low], fifth, row)
        give(2)
        give(6)
    else:
        for o in far_first(nz):
            give(o)
    send(BS, 0, basis, v_basis, z, (row + n_row - 1) % n_row)

    for load in loads[3:]:
        load.wait()
    step = 256

    def apply_inverse(t, carried):
        at = pl.ds(pl.multiple_of(t * step, step), step)
        v_app[at, :] = mm(v_inv[at, :], v_rhs[...]).astype(BF16)
        return carried

    lax.fori_loop(0, order // step, apply_inverse, 0)
    for t in range(order // step):
        v_invt[:, t * step : (t + 1) * step] = v_inv[t * step : (t + 1) * step, :].T
    inc_t[...] = v_inc[...].T.reshape(inc_t.shape)
    if merging:
        await_slot(ME, 0, merge_in.at[0])
        merged[0] = merge_in[0] + part[third, :thin, :]
        send(RS, 3, merged.at[0], part_in.at[z, low], third, row)
        await_slot(ME, 1, merge_in.at[1])
        merged[1] = merge_in[1] + part[fifth, thin:, :]
        send(RS, 5, merged.at[1], part_in.at[z, high_rows], fifth, row)
        give(1)
        give(7)

    await_slot(BS, 0, v_basis)
    step_shift = mm(v_basis[...], v_app[...], 0, 0)
    shift[...] = step_shift.T.reshape(shift.shape)
    for o in range(1, ni):
        peer = (i + o) % ni
        send(SH, o, shift.at[peer], shift_in.at[i], z, rows + peer)
    shift_in[i] = shift[i]

    summed = part[z]
    givers = [o for o in far_first(nz)[::-1] if not (merging and o == 4)]
    await_slot(RS, 0, part_in.at[pl.ds(0, len(givers))])
    for o in givers:
        summed = summed + part_in[(z + nz - o) % nz]
    range_t = (-summed).astype(BF16)
    gain_part = mm(range_t, v_invt[...]).astype(BF16)
    gain_t[z] = gain_part
    high, low = split(-mm(gain_part, v_basis[...]))
    maps[i, z] = jnp.concatenate([high, low], axis=1)
    for o in far_first(nz):
        send(MZ, o, maps.at[i, z], maps.at[i, z], (z + o) % nz, row)

    def spread(layer):
        for o in far_first(ni):
            send(MI, o, maps.at[i, layer], maps.at[i, layer], z, rows + (i + o) % ni)

    spread(z)
    for o in far_first(nz)[::-1]:
        source = (z + nz - o) % nz
        await_slot(MZ, o, maps.at[i, source])
        spread(source)
    for o in far_first(nz):
        send(GZ, o, gain_t.at[z], gain_t.at[z], (z + o) % nz, row)

    await_slot(SH, 0, shift_in.at[pl.ds(0, ni - 1)])

    def arrive(k):
        @pl.when(k != i)
        def _():
            await_slot(MI, (i + ni - k) % ni, maps.at[k])

    arrive(0)
    first = maps[0].reshape(rank, 2 * rank).astype(F32)
    state = jnp.concatenate([shift_in[0], first[:, :rank] + first[:, rank:]], axis=0)
    tall = cols + rank
    for k in range(1, ni):
        pre_s[k] = state[:cols]
        pre_m[:, k * rank : (k + 1) * rank] = state[cols:].astype(BF16)
        arrive(k)
        product = mm(jnp.concatenate(split(state), axis=0), maps[k].reshape(rank, 2 * rank))
        state = product[:tall, :rank] + (product[:tall, rank:] + product[tall:, :rank])
        state = jnp.concatenate([state[:cols] + shift_in[k], state[cols:]], axis=0)
    half = rank // 2
    shifts, core = pl.ds(half, cols), i % 2
    mine = pl.ds(pl.multiple_of(core * half, half), half + cols)
    map_mine = pl.ds(pl.multiple_of(core * (half + cols), half), half)
    total[:half, :] = state[cols : cols + half].astype(BF16)
    total[half : half + cols, :] = state[:cols].astype(BF16)
    total[half + cols :, :] = state[cols + half :].astype(BF16)
    carry[...] = inc_t[i]

    def matrix_of(rows):
        return jnp.concatenate([rows[:half], rows[half + cols :]], axis=0)

    def outer_copies(act):
        for d in far_first(ny):

            @pl.when(y == 0)
            def _():
                act(d, total.at[shifts], total_in.at[d, shifts])

            @pl.when(jnp.logical_and(y > 0, y + d < ny))
            def _():
                act(d, total.at[mine], total_in.at[d, mine])

    @pl.when(y == 0)
    def _():
        product = mm(jnp.concatenate(split(carry[...]), axis=0), matrix_of(total[...]))
        total[half : half + cols, :] = (product[:cols] + product[cols:] + state[:cols]).astype(BF16)

    def outer_sent(d, source, target):
        pltpu.make_async_remote_copy(
            src_ref=source,
            dst_ref=target,
            **semaphores(OU, d),
            device_id=(z, row + d * ni),
            device_id_type=MESH,
        ).wait_send()

    outer_copies(lambda d, source, target: send(OU, d, source, target, z, row + d * ni))

    def forward(d):
        return pltpu.make_async_remote_copy(
            src_ref=total_in.at[d, map_mine],
            dst_ref=total_in.at[d, map_mine],
            **semaphores(FW, d),
            device_id=(z, row + 1 - 2 * core),
            device_id_type=MESH,
        )

    for d in range(1, ny):

        @pl.when(d < y)
        def _():
            await_slot(OU, d, total_in.at[d, mine])
            forward(d).start()

        near = d - 1
        if near < 1:
            continue

        @pl.when(near < y)
        def _():
            forward(near).wait_recv()
            matrix = matrix_of(total_in[near])
            if near == 1:
                block[:cols, :] = total_in[near, half : half + cols, :].astype(F32)
                block[cols:, :] = matrix.astype(F32)
            else:
                rows_in = jnp.concatenate([total_in[near, half : half + cols, :], matrix], axis=0)
                product = mm(rows_in, jnp.concatenate(split(block[cols:, :]), axis=1))
                product = product[:, :rank] + product[:, rank:]
                block[:cols, :] += product[:cols]
                block[cols:, :] = product[cols:]

    for d in range(1, ny):

        @pl.when(d == y)
        def _():
            await_slot(OU, d, total_in.at[d, shifts])
            if d == 1:
                carry[...] = total_in[d, half : half + cols, :].astype(F32)
            else:
                product = mm(total_in[d, half : half + cols, :], jnp.concatenate(split(block[cols:, :]), axis=1))
                carry[...] = product[:, :rank] + product[:, rank:] + block[:cols, :]

    start = carry[...]
    coup[0] = start.astype(BF16)
    product = mm(jnp.concatenate(split(start), axis=0), pre_m[:, rank:])
    product = product[:cols] + product[cols:]
    for k in range(1, ni):
        coup[k] = (product[:, (k - 1) * rank : k * rank] + pre_s[k]).astype(BF16)
    for o in far_first(ni):
        peer = (i + o) % ni
        send(CB, o, coup.at[peer], coup_in.at[i], z, rows + peer)
    coup_in[i] = coup[i]
    await_slot(GZ, 0, gain_t.at[pl.ds(0, nz - 1)])
    gain[...] = gain_t[...].reshape(rank, order).T
    await_slot(CB, 0, coup_in.at[pl.ds(0, ni - 1)])

    coupled_t = coup_in[...].reshape(width, rank)
    for t in range(order // step):
        at = slice(t * step, (t + 1) * step)
        out[at, :] = (v_app[at, :].astype(F32) - mm(gain[at, :], coupled_t, 1, 1)).astype(BF16)

    def drain(kind, source):
        pltpu.make_async_remote_copy(
            src_ref=source,
            dst_ref=source,
            **semaphores(kind, 0),
            device_id=(z, row),
            device_id_type=MESH,
        ).wait_send()

    drain(RS, part.at[pl.ds(0, len(givers))])
    if merging:
        drain(ME, merged)
    drain(BS, v_basis)
    drain(SH, shift.at[pl.ds(0, ni - 1)])
    drain(MZ, maps.at[i, pl.ds(0, nz - 1)])
    drain(MI, maps.at[pl.ds(0, ni - 1)])
    drain(GZ, gain_t.at[pl.ds(0, nz - 1)])
    drain(CB, coup.at[pl.ds(0, ni - 1)])
    outer_copies(outer_sent)
    for d in range(1, ny - 1):

        @pl.when(d < y)
        def _():
            forward(d).wait_send()


def solution(mesh, inner=INNER):
    nz, n_row = mesh.shape["layer"], mesh.shape["row"]
    ni, ny = inner, n_row // inner

    def body(left, right, sketch, row_basis, inverse, rhs, incoming):
        order, rank = sketch.shape
        width = rhs.shape[1]
        cols, thick = width // ni, rank // nz
        vm = pltpu.VMEM
        return pl.pallas_call(
            functools.partial(kernel, nz, ni, ny),
            out_shape=jax.ShapeDtypeStruct((order, width), BF16),
            in_specs=[pl.BlockSpec(memory_space=pltpu.HBM)] * 7,
            out_specs=pl.BlockSpec(memory_space=pltpu.VMEM),
            scratch_shapes=[
                vm((order, rank), BF16),
                vm((order, rank), BF16),
                vm((order, rank), BF16),
                vm((order, rank), BF16),
                vm((order, order), BF16),
                vm((order, order), BF16),
                vm((order, width), BF16),
                vm((rank, width), F32),
                vm((order, width), BF16),
                vm((nz, thick, order), F32),
                vm((nz, thick, order), F32),
                vm((ni, cols, rank), F32),
                vm((ni, cols, rank), F32),
                vm((ni, nz, thick, 2 * rank), BF16),
                vm((nz, thick, order), BF16),
                vm((order, rank), BF16),
                vm((ni, cols, rank), F32),
                vm((rank, ni * rank), BF16),
                vm((cols + rank, rank), BF16),
                vm((ny, cols + rank, rank), BF16),
                vm((ni, cols, rank), F32),
                vm((cols, rank), F32),
                vm((ni, cols, rank), BF16),
                vm((ni, cols, rank), BF16),
                vm((cols + rank, rank), F32),
                vm((2, max(thick // 2, 8), order), F32),
                vm((2, max(thick // 2, 8), order), F32),
                pltpu.SemaphoreType.DMA((6,)),
                pltpu.SemaphoreType.DMA((24,)),
                pltpu.SemaphoreType.DMA((39,)),
            ],
            compiler_params=pltpu.CompilerParams(
                collective_id=0, has_side_effects=True, vmem_limit_bytes=48 << 20
            ),
        )(*[pltpu.with_memory_space_constraint(a, pltpu.HBM) for a in (left[0], right[0], sketch, row_basis, inverse, rhs, incoming)])

    return jax.shard_map(
        body,
        mesh=mesh,
        in_specs=(
            P("layer", "row", None),
            P("layer", "row", None),
            P("row", None),
            P("row", None),
            P("row", None),
            P("row", "layer"),
            P(None, "layer"),
        ),
        out_specs=P("row", "layer"),
        check_vma=False,
    )
```

```python
import functools

import jax
import jax.numpy as jnp
from jax import lax
from jax.experimental import pallas as pl
from jax.experimental.pallas import tpu as pltpu
from jax.sharding import PartitionSpec as P

MESH = pl.DeviceIdType.MESH
INNER = 8
BF16 = jnp.bfloat16
F32 = jnp.float32


def mm(a, b, ca=1, cb=0):
    return lax.dot_general(a, b, (((ca,), (cb,)), ((), ())), preferred_element_type=F32)


def split(value):
    high = value.astype(BF16)
    return high, (value - high.astype(F32)).astype(BF16)


def far_first(n):
    return sorted(range(1, n), key=lambda o: -min(o, n - o))


RS, SH, GZ, CB, BS, ME, MZ, MI, OU, FW = range(10)
SEND_AT = [0, 1, 2, 3, 4, 5, 6, 7, 8, 16]
RECV_AT = [0, 1, 2, 3, 4, 5, 7, 15, 23, 31]


def kernel(
    nz, ni, ny,
    left, right, sketch, basis, inverse, rhs, incoming,
    out,
    v_left, v_right, v_sketch, v_basis, v_inv, v_invt, v_rhs, v_inc, v_app,
    part, part_in, shift, shift_in, maps, gain_t, gain, pre_s, pre_m, total, total_in,
    inc_t, carry, coup, coup_in,
    block, merge_in, merged, load_sem, send_sem, recv_sem,
):
    z, row = lax.axis_index("layer"), lax.axis_index("row")
    y, i = row // ni, row % ni
    rows = row - i
    n_row = ni * ny
    order, rank = v_inv.shape[0], v_sketch.shape[1]
    width = v_rhs.shape[1]
    cols = width // ni
    thick = rank // nz

    barrier = pltpu.get_barrier_semaphore()

    def greet(layer, target):
        pl.semaphore_signal(barrier, inc=1, device_id=(layer, target), device_id_type=MESH)

    for o in range(1, nz):
        greet((z + o) % nz, row)
    for o in range(1, ni):
        greet(z, rows + (i + o) % ni)
    for o in range(1, ny):
        greet(z, ((y + o) % ny) * ni + i)
    greet(z, (row + 1) % n_row)
    greet(z, (row + n_row - 1) % n_row)

    loads = [
        pltpu.make_async_copy(source, target, load_sem.at[k])
        for k, (source, target) in enumerate(
            [(right, v_right), (sketch, v_sketch), (left, v_left), (inverse, v_inv), (rhs, v_rhs), (incoming, v_inc)]
        )
    ]
    for load in loads:
        load.start()

    def semaphores(kind, slot):
        sent_at = SEND_AT[kind] + (slot if kind in (OU, FW) else 0)
        got_at = RECV_AT[kind] + (slot if kind in (ME, MZ, MI, OU, FW) else 0)
        return {"send_sem": send_sem.at[sent_at], "recv_sem": recv_sem.at[got_at]}

    def send(kind, slot, source, target, layer, dest):
        copy = pltpu.make_async_remote_copy(
            src_ref=source,
            dst_ref=target,
            **semaphores(kind, slot),
            device_id=(layer, dest),
            device_id_type=MESH,
        )
        copy.start()
        return copy

    def await_slot(kind, slot, target):
        pltpu.make_async_remote_copy(
            src_ref=target,
            dst_ref=target,
            **semaphores(kind, slot),
            device_id=(z, row),
            device_id_type=MESH,
        ).wait_recv()

    loads[0].wait()
    loads[1].wait()
    core_t = mm(v_sketch[...], v_right[...], 0, 0).astype(BF16)
    loads[2].wait()
    part[...] = mm(core_t, v_left[...], 1, 1).reshape(part.shape)

    pl.semaphore_wait(barrier, (nz - 1) + (ni - 1) + (ny - 1) + 2)

    merging = nz == 8
    thin = thick // 2
    low, high_rows = pl.ds(0, thin), pl.ds(thin, thin)

    def give(o):
        peer = (z + o) % nz
        send(RS, o, part.at[peer], part_in.at[z], peer, row)

    if merging:
        across = (z + 4) % nz
        send(ME, 0, part.at[across, low], merge_in.at[0], (z + 1) % nz, row)
        send(ME, 1, part.at[across, high_rows], merge_in.at[1], (z + 7) % nz, row)
        third, fifth = (z + 3) % nz, (z + 5) % nz
        send(RS, 3, part.at[third, high_rows], part_in.at[z, high_rows], third, row)
        send(RS, 5, part.at[fifth, low], part_in.at[z, low], fifth, row)
        give(2)
        give(6)
    else:
        for o in far_first(nz):
            give(o)
    send(BS, 0, basis, v_basis, z, (row + n_row - 1) % n_row)

    for load in loads[3:]:
        load.wait()
    step = 256

    def apply_inverse(t, carried):
        at = pl.ds(pl.multiple_of(t * step, step), step)
        v_app[at, :] = mm(v_inv[at, :], v_rhs[...]).astype(BF16)
        return carried

    lax.fori_loop(0, order // step, apply_inverse, 0)
    for t in range(order // step):
        v_invt[:, t * step : (t + 1) * step] = v_inv[t * step : (t + 1) * step, :].T
    inc_t[...] = v_inc[...].T.reshape(inc_t.shape)
    if merging:
        await_slot(ME, 0, merge_in.at[0])
        merged[0] = merge_in[0] + part[third, :thin, :]
        send(RS, 3, merged.at[0], part_in.at[z, low], third, row)
        await_slot(ME, 1, merge_in.at[1])
        merged[1] = merge_in[1] + part[fifth, thin:, :]
        send(RS, 5, merged.at[1], part_in.at[z, high_rows], fifth, row)
        give(1)
        give(7)

    await_slot(BS, 0, v_basis)
    step_shift = mm(v_basis[...], v_app[...], 0, 0)
    shift[...] = step_shift.T.reshape(shift.shape)
    for o in range(1, ni):
        peer = (i + o) % ni
        send(SH, o, shift.at[peer], shift_in.at[i], z, rows + peer)
    shift_in[i] = shift[i]

    summed = part[z]
    givers = [o for o in far_first(nz)[::-1] if not (merging and o == 4)]
    await_slot(RS, 0, part_in.at[pl.ds(0, len(givers))])
    for o in givers:
        summed = summed + part_in[(z + nz - o) % nz]
    range_t = (-summed).astype(BF16)
    gain_part = mm(range_t, v_invt[...]).astype(BF16)
    gain_t[z] = gain_part
    high, low = split(-mm(gain_part, v_basis[...]))
    maps[i, z] = jnp.concatenate([high, low], axis=1)
    for o in far_first(nz):
        send(MZ, o, maps.at[i, z], maps.at[i, z], (z + o) % nz, row)

    def spread(layer):
        for o in far_first(ni):
            send(MI, o, maps.at[i, layer], maps.at[i, layer], z, rows + (i + o) % ni)

    spread(z)
    for o in far_first(nz)[::-1]:
        source = (z + nz - o) % nz
        await_slot(MZ, o, maps.at[i, source])
        spread(source)
    for o in far_first(nz):
        send(GZ, o, gain_t.at[z], gain_t.at[z], (z + o) % nz, row)

    await_slot(SH, 0, shift_in.at[pl.ds(0, ni - 1)])

    def arrive(k):
        @pl.when(k != i)
        def _():
            await_slot(MI, (i + ni - k) % ni, maps.at[k])

    arrive(0)
    first = maps[0].reshape(rank, 2 * rank).astype(F32)
    state = jnp.concatenate([shift_in[0], first[:, :rank] + first[:, rank:]], axis=0)
    tall = cols + rank
    for k in range(1, ni):
        pre_s[k] = state[:cols]
        pre_m[:, k * rank : (k + 1) * rank] = state[cols:].astype(BF16)
        arrive(k)
        product = mm(jnp.concatenate(split(state), axis=0), maps[k].reshape(rank, 2 * rank))
        state = product[:tall, :rank] + (product[:tall, rank:] + product[tall:, :rank])
        state = jnp.concatenate([state[:cols] + shift_in[k], state[cols:]], axis=0)
    half = rank // 2
    shifts, core = pl.ds(half, cols), i % 2
    mine = pl.ds(pl.multiple_of(core * half, half), half + cols)
    map_mine = pl.ds(pl.multiple_of(core * (half + cols), half), half)
    total[:half, :] = state[cols : cols + half].astype(BF16)
    total[half : half + cols, :] = state[:cols].astype(BF16)
    total[half + cols :, :] = state[cols + half :].astype(BF16)
    carry[...] = inc_t[i]

    def matrix_of(rows):
        return jnp.concatenate([rows[:half], rows[half + cols :]], axis=0)

    def outer_copies(act):
        for d in far_first(ny):

            @pl.when(y == 0)
            def _():
                act(d, total.at[shifts], total_in.at[d, shifts])

            @pl.when(jnp.logical_and(y > 0, y + d < ny))
            def _():
                act(d, total.at[mine], total_in.at[d, mine])

    @pl.when(y == 0)
    def _():
        product = mm(jnp.concatenate(split(carry[...]), axis=0), matrix_of(total[...]))
        total[half : half + cols, :] = (product[:cols] + product[cols:] + state[:cols]).astype(BF16)

    def outer_sent(d, source, target):
        pltpu.make_async_remote_copy(
            src_ref=source,
            dst_ref=target,
            **semaphores(OU, d),
            device_id=(z, row + d * ni),
            device_id_type=MESH,
        ).wait_send()

    outer_copies(lambda d, source, target: send(OU, d, source, target, z, row + d * ni))

    def forward(d):
        return pltpu.make_async_remote_copy(
            src_ref=total_in.at[d, map_mine],
            dst_ref=total_in.at[d, map_mine],
            **semaphores(FW, d),
            device_id=(z, row + 1 - 2 * core),
            device_id_type=MESH,
        )

    for d in far_first(ny):

        @pl.when(d < y)
        def _():
            await_slot(OU, d, total_in.at[d, mine])
            forward(d).start()

    for near in range(1, ny - 1):

        @pl.when(near < y)
        def _():
            forward(near).wait_recv()
            matrix = matrix_of(total_in[near])
            if near == 1:
                block[:cols, :] = total_in[near, half : half + cols, :].astype(F32)
                block[cols:, :] = matrix.astype(F32)
            else:
                rows_in = jnp.concatenate([total_in[near, half : half + cols, :], matrix], axis=0)
                product = mm(rows_in, jnp.concatenate(split(block[cols:, :]), axis=1))
                product = product[:, :rank] + product[:, rank:]
                block[:cols, :] += product[:cols]
                block[cols:, :] = product[cols:]

    for d in range(1, ny):

        @pl.when(d == y)
        def _():
            await_slot(OU, d, total_in.at[d, shifts])
            if d == 1:
                carry[...] = total_in[d, half : half + cols, :].astype(F32)
            else:
                product = mm(total_in[d, half : half + cols, :], jnp.concatenate(split(block[cols:, :]), axis=1))
                carry[...] = product[:, :rank] + product[:, rank:] + block[:cols, :]

    start = carry[...]
    coup[0] = start.astype(BF16)
    product = mm(jnp.concatenate(split(start), axis=0), pre_m[:, rank:])
    product = product[:cols] + product[cols:]
    for k in range(1, ni):
        coup[k] = (product[:, (k - 1) * rank : k * rank] + pre_s[k]).astype(BF16)
    for o in far_first(ni):
        peer = (i + o) % ni
        send(CB, o, coup.at[peer], coup_in.at[i], z, rows + peer)
    coup_in[i] = coup[i]
    await_slot(GZ, 0, gain_t.at[pl.ds(0, nz - 1)])
    gain[...] = gain_t[...].reshape(rank, order).T
    await_slot(CB, 0, coup_in.at[pl.ds(0, ni - 1)])

    coupled_t = coup_in[...].reshape(width, rank)
    for t in range(order // step):
        at = slice(t * step, (t + 1) * step)
        out[at, :] = (v_app[at, :].astype(F32) - mm(gain[at, :], coupled_t, 1, 1)).astype(BF16)

    def drain(kind, source):
        pltpu.make_async_remote_copy(
            src_ref=source,
            dst_ref=source,
            **semaphores(kind, 0),
            device_id=(z, row),
            device_id_type=MESH,
        ).wait_send()

    drain(RS, part.at[pl.ds(0, len(givers))])
    if merging:
        drain(ME, merged)
    drain(BS, v_basis)
    drain(SH, shift.at[pl.ds(0, ni - 1)])
    drain(MZ, maps.at[i, pl.ds(0, nz - 1)])
    drain(MI, maps.at[pl.ds(0, ni - 1)])
    drain(GZ, gain_t.at[pl.ds(0, nz - 1)])
    drain(CB, coup.at[pl.ds(0, ni - 1)])
    outer_copies(outer_sent)
    for d in range(1, ny - 1):

        @pl.when(d < y)
        def _():
            forward(d).wait_send()


def solution(mesh, inner=INNER):
    nz, n_row = mesh.shape["layer"], mesh.shape["row"]
    ni, ny = inner, n_row // inner

    def body(left, right, sketch, row_basis, inverse, rhs, incoming):
        order, rank = sketch.shape
        width = rhs.shape[1]
        cols, thick = width // ni, rank // nz
        vm = pltpu.VMEM
        return pl.pallas_call(
            functools.partial(kernel, nz, ni, ny),
            out_shape=jax.ShapeDtypeStruct((order, width), BF16),
            in_specs=[pl.BlockSpec(memory_space=pltpu.HBM)] * 7,
            out_specs=pl.BlockSpec(memory_space=pltpu.VMEM),
            scratch_shapes=[
                vm((order, rank), BF16),
                vm((order, rank), BF16),
                vm((order, rank), BF16),
                vm((order, rank), BF16),
                vm((order, order), BF16),
                vm((order, order), BF16),
                vm((order, width), BF16),
                vm((rank, width), F32),
                vm((order, width), BF16),
                vm((nz, thick, order), F32),
                vm((nz, thick, order), F32),
                vm((ni, cols, rank), F32),
                vm((ni, cols, rank), F32),
                vm((ni, nz, thick, 2 * rank), BF16),
                vm((nz, thick, order), BF16),
                vm((order, rank), BF16),
                vm((ni, cols, rank), F32),
                vm((rank, ni * rank), BF16),
                vm((cols + rank, rank), BF16),
                vm((ny, cols + rank, rank), BF16),
                vm((ni, cols, rank), F32),
                vm((cols, rank), F32),
                vm((ni, cols, rank), BF16),
                vm((ni, cols, rank), BF16),
                vm((cols + rank, rank), F32),
                vm((2, max(thick // 2, 8), order), F32),
                vm((2, max(thick // 2, 8), order), F32),
                pltpu.SemaphoreType.DMA((6,)),
                pltpu.SemaphoreType.DMA((24,)),
                pltpu.SemaphoreType.DMA((39,)),
            ],
            compiler_params=pltpu.CompilerParams(
                collective_id=0, has_side_effects=True, vmem_limit_bytes=48 << 20
            ),
        )(*[pltpu.with_memory_space_constraint(a, pltpu.HBM) for a in (left[0], right[0], sketch, row_basis, inverse, rhs, incoming)])

    return jax.shard_map(
        body,
        mesh=mesh,
        in_specs=(
            P("layer", "row", None),
            P("layer", "row", None),
            P("row", None),
            P("row", None),
            P("row", None),
            P("row", "layer"),
            P(None, "layer"),
        ),
        out_specs=P("row", "layer"),
        check_vma=False,
    )
```
